32 devices in a mesh: gx: 4 (over z), gy: 8 (over y, x, core).
Axes of the slice: x: 2, y: 2, z: 4, core: 2. Of those that a mesh axis runs over, the one named last changes fastest.
Arguments:
- offsets: float32 [2, 16, 32, 256], P(None, 'gx', 'gy'), may hold values from 0 to 1
- probes: float32 [16, 16, 32, 256], P(None, 'gx', 'gy'), may hold values from -6 to 6
- counts: int32 [16, 32], P('gx', 'gy'), may hold values from 1 to 256, as said below
Outputs:
- kernel_product: float32 [16, 16, 32, 256], P(None, 'gx', 'gy')
The draws below stay inside these ranges and needn't reach their ends.
Inputs may be any that keep to these rules, and one draw needn't show every extreme that they name: `counts`: each draw has a leaf with all 256 slots used and a leaf with one slot used.
All inputs are finite; a program needn't handle non-finite values.
Results may differ from the reference program's by a relative error of at most 0.0001.
Values sent between devices are 32-bit elements; how exact they have to be, the bound alone decides.
A program may use at most 64 MiB of HBM per device.

```python
import jax
import jax.numpy as jnp
from jax import lax

ORDER = 8
LEAF = 256
PROBES = 16
DEPTH = 2
NXL = 16
NYL = 32


def draw_counts(key, part):
    key_level, key_full, key_single = jax.random.split(key, 3)
    spread = jax.random.randint(key_level, (NXL, NYL), 0, LEAF)
    counts = LEAF - spread * spread // LEAF
    cells = jnp.arange(NXL * NYL, dtype=jnp.int32).reshape(NXL, NYL)
    full_cell = jax.random.randint(key_full, (), 0, NXL * NYL)
    single_cell = (full_cell + 1 + jax.random.randint(key_single, (), 0, NXL * NYL - 1)) % (NXL * NYL)
    counts = jnp.where(cells == full_cell, LEAF, counts)
    counts = jnp.where(cells == single_cell, 1, counts)
    return counts.astype(jnp.int32)


def shard_levels(own_key, shape, cuts, smallest, largest):
    factor_of = 1.0
    for dim, shards_of in cuts:
        steps = jax.random.uniform(jax.random.fold_in(jax.random.fold_in(own_key, 6), dim), (shards_of,), jnp.float32, smallest / len(cuts), largest / len(cuts))
        factor_of = factor_of * jnp.repeat(jnp.exp(steps), shape[dim] // shards_of).reshape((-1,) + (1,) * (len(shape) - 1 - dim))
    return factor_of


def bell_draw(key, shape, scale, limit, shards=(), held_as=jnp.bfloat16):
    factor_of = shard_levels(key, shape, shards, -0.22, 0.18) if shards else 1.0
    entries = jax.random.normal(key, shape, jnp.float32) * scale * factor_of
    return jnp.minimum(jnp.maximum(entries, -limit), limit).astype(held_as)


def setup_inputs(seed: int = 0) -> dict:
    streams_of = jax.random.split(jax.random.key(seed), 4)
    offsets = jnp.clip(1.0 * jax.random.uniform(streams_of[0], (2, NXL, NYL, LEAF), jnp.float32) ** shard_levels(streams_of[0], (2, NXL, NYL, LEAF), ((1, 4), (2, 8)), -0.2, 0.2), 0.0, 1.0)
    probes = bell_draw(streams_of[1], (PROBES, NXL, NYL, LEAF), 1.0, 6.0, ((1, 4), (2, 8)), jnp.float32)
    counts = draw_counts(jax.random.fold_in(streams_of[3], 71), 0)
    return dict(offsets=offsets, probes=probes, counts=counts)


ROOT_THREE = 1.7320508075688772
LENGTH_SCALE = 6.0
AMPLITUDE = 1.0 / 96.0
SHORT_LENGTH = 0.5
SHORT_AMPLITUDE = 1.0 / 16.0
NUGGET = 0.5

def matern(dist_sq):
    distance = jnp.sqrt(dist_sq)
    scaled = ROOT_THREE * distance / LENGTH_SCALE
    short_scaled = ROOT_THREE * distance / SHORT_LENGTH
    long_part = AMPLITUDE * (1.0 + scaled) * jnp.exp(-scaled)
    return long_part + SHORT_AMPLITUDE * (1.0 + short_scaled) * jnp.exp(-short_scaled)

def cheb_nodes(degree):
    node_slots = jnp.arange(degree, dtype=jnp.float32)
    return jnp.cos((2.0 * node_slots + 1.0) * (jnp.pi / (2.0 * degree)))

def cheb_weights(coords, degree):
    powers = jnp.arange(1, degree, dtype=jnp.float32)
    node_slots = jnp.arange(degree, dtype=jnp.float32)
    angles = jnp.arccos(jnp.clip(coords, -1.0, 1.0))
    series = jnp.cos(angles[..., None] * powers)
    at_nodes = jnp.cos(powers[:, None] * (2.0 * node_slots[None, :] + 1.0) * (jnp.pi / (2.0 * degree)))
    return 1.0 / degree + 2.0 / degree * jnp.einsum('...k,km->...m', series, at_nodes, precision=lax.Precision.HIGHEST)

def leaf_weights(offsets, degree):
    along_x = cheb_weights(2.0 * offsets[0] - 1.0, degree)
    along_y = cheb_weights(2.0 * offsets[1] - 1.0, degree)
    product = along_x[..., :, None] * along_y[..., None, :]
    return product.reshape(offsets.shape[1:] + (degree * degree,))

def child_maps(degree):
    node_values = cheb_nodes(degree)
    result = []
    for child_x in range(2):
        for child_y in range(2):
            weight_x = cheb_weights((node_values - 1.0) / 2.0 + child_x, degree)
            weight_y = cheb_weights((node_values - 1.0) / 2.0 + child_y, degree)
            result.append((weight_x[:, None, :, None] * weight_y[None, :, None, :]).reshape(degree * degree, degree * degree))
    return jnp.stack(result).reshape(2, 2, degree * degree, degree * degree)

def upward(children, maps_table):
    half_x = children.shape[0] // 2
    half_y = children.shape[1] // 2
    grouped = children.reshape((half_x, 2, half_y, 2) + children.shape[2:])
    return jnp.einsum('xyrq,ixjypr->ijpq', maps_table, grouped, precision=lax.Precision.HIGHEST)

def downward(parents, maps_table):
    spread = jnp.einsum('xyrq,ijpq->ixjypr', maps_table, parents, precision=lax.Precision.HIGHEST)
    return spread.reshape((2 * parents.shape[0], 2 * parents.shape[1]) + parents.shape[2:])

def transfer_kernel(shift_x, shift_y, box_side, degree):
    node_values = cheb_nodes(degree) * (box_side / 2.0)
    node_x = jnp.repeat(node_values, degree)
    node_y = jnp.tile(node_values, degree)
    delta_x = node_x[:, None] - node_x[None, :] - jnp.asarray(shift_x)[..., None, None] * box_side
    delta_y = node_y[:, None] - node_y[None, :] - jnp.asarray(shift_y)[..., None, None] * box_side
    return matern(delta_x * delta_x + delta_y * delta_y)

def interact(window, count_x, count_y, base_x, base_y, box_side, degree):
    cells_x = base_x + jnp.arange(count_x, dtype=jnp.int32)
    cells_y = base_y + jnp.arange(count_y, dtype=jnp.int32)
    accumulated = jnp.zeros((count_x, count_y) + window.shape[2:], jnp.float32)
    for a in range(-3, 4):
        for b in range(-3, 4):
            if max(abs(a), abs(b)) < 2:
                continue
            within_x = jnp.abs((cells_x + a) // 2 - cells_x // 2) <= 1
            within_y = jnp.abs((cells_y + b) // 2 - cells_y // 2) <= 1
            allowed = (within_x[:, None] & within_y[None, :]).astype(jnp.float32)
            matrix = transfer_kernel(jnp.float32(a), jnp.float32(b), box_side, degree)
            source = window[3 + a:3 + a + count_x, 3 + b:3 + b + count_y]
            accumulated = accumulated + allowed[:, :, None, None] * jnp.einsum('qr,ijpr->ijpq', matrix, source, precision=lax.Precision.HIGHEST)
    return accumulated

def interact_top(box_grid, own_x, own_y, box_side, degree):
    shift_x = (jnp.arange(box_grid.shape[0], dtype=jnp.int32) - own_x).astype(jnp.float32)
    shift_y = (jnp.arange(box_grid.shape[1], dtype=jnp.int32) - own_y).astype(jnp.float32)
    spread_x = shift_x[:, None] + 0.0 * shift_y[None, :]
    spread_y = 0.0 * shift_x[:, None] + shift_y[None, :]
    matrices = transfer_kernel(spread_x, spread_y, box_side, degree)
    separated = (jnp.maximum(jnp.abs(spread_x), jnp.abs(spread_y)) >= 2.0).astype(jnp.float32)
    return jnp.einsum('abqr,abpr->pq', matrices * separated[:, :, None, None], box_grid, precision=lax.Precision.HIGHEST)

def near_row(window, targets):
    width = targets.shape[1]
    accumulated = jnp.zeros((window.shape[0] - 2, width, targets.shape[2]), jnp.float32)
    for a in range(3):
        for b in range(3):
            source = window[:, a, b:b + width]
            delta_x = targets[0][:, :, None] - source[0][:, None, :] - (a - 1.0)
            delta_y = targets[1][:, :, None] - source[1][:, None, :] - (b - 1.0)
            kernel_tile = matern(delta_x * delta_x + delta_y * delta_y)
            accumulated = accumulated + jnp.einsum('jst,pjt->pjs', kernel_tile, source[2:], precision=lax.Precision.HIGHEST)
    return accumulated

def near_field(padded, offsets):

    def one_row(row_index):
        window = lax.dynamic_slice_in_dim(padded, row_index, 3, 1)
        targets = lax.dynamic_index_in_dim(offsets, row_index, 1, keepdims=False)
        return near_row(window, targets)
    row_terms = lax.map(one_row, jnp.arange(offsets.shape[1], dtype=jnp.int32))
    return jnp.transpose(row_terms, (1, 0, 2, 3))

def reference(offsets, probes, counts):
    degree = ORDER
    in_use = (jnp.arange(LEAF, dtype=jnp.int32)[None, None, :] < counts[:, :, None]).astype(jnp.float32)
    masked = probes * in_use[None]
    stacked = jnp.concatenate([offsets, masked], axis=0)
    padded = jnp.pad(stacked, ((0, 0), (1, 1), (1, 1), (0, 0)))
    near_part = near_field(padded, offsets)
    weights = leaf_weights(offsets, degree)
    maps_table = child_maps(degree)
    levels = [jnp.einsum('ijsq,pijs->ijpq', weights, masked, precision=lax.Precision.HIGHEST)]
    top_level = DEPTH + 2
    for repeat in range(top_level):
        levels.append(upward(levels[-1], maps_table))
    box_grid = levels[top_level]
    grid_rows = []
    for box_x in range(box_grid.shape[0]):
        grid_cols = [interact_top(box_grid, box_x, box_y, 2.0 ** top_level, degree) for box_y in range(box_grid.shape[1])]
        grid_rows.append(jnp.stack(grid_cols))
    local_exp = jnp.stack(grid_rows)
    for level_index in range(top_level - 1, -1, -1):
        source = jnp.pad(levels[level_index], ((3, 3), (3, 3), (0, 0), (0, 0)))
        local_exp = downward(local_exp, maps_table) + interact(source, levels[level_index].shape[0], levels[level_index].shape[1], 0, 0, 2.0 ** level_index, degree)
    far_part = jnp.einsum('ijsq,ijpq->pijs', weights, local_exp, precision=lax.Precision.HIGHEST)
    return in_use[None] * (near_part + far_part + NUGGET * masked)
```

```python
import functools
import math

import jax
import jax.numpy as jnp
import numpy as np
from jax import lax
from jax.experimental import pallas as pl
from jax.experimental.pallas import tpu as pltpu
from jax.sharding import PartitionSpec as P

ORDER = 8
NODES = ORDER * ORDER
ROOT_THREE = 1.7320508075688772
LENGTH_SCALE = 6.0
AMPLITUDE = 1.0 / 96.0
SHORT_AMPLITUDE = 1.0 / 16.0
NUGGET = 0.5
RATIO = 12
UNIT = ROOT_THREE / LENGTH_SCALE
HIGH = lax.Precision.HIGH
HIGHEST = lax.Precision.HIGHEST
ROWS = 24


def node_table():
    slots = np.arange(ORDER)
    return np.cos((2.0 * slots + 1.0) * (np.pi / (2.0 * ORDER)))


def series_at_nodes():
    powers = np.arange(ORDER)
    slots = np.arange(ORDER)
    table = np.cos(powers[:, None] * (2.0 * slots[None, :] + 1.0) * (np.pi / (2.0 * ORDER)))
    table = table * (2.0 / ORDER)
    table[0] = 1.0 / ORDER
    return table


def interpolation(coords):
    angles = np.arccos(np.clip(coords, -1.0, 1.0))
    series = np.cos(angles[:, None] * np.arange(ORDER))
    return series @ series_at_nodes()


def child_maps():
    nodes = node_table()
    result = []
    for child_x in range(2):
        for child_y in range(2):
            weight_x = interpolation((nodes - 1.0) / 2.0 + child_x)
            weight_y = interpolation((nodes - 1.0) / 2.0 + child_y)
            result.append(
                (weight_x[:, None, :, None] * weight_y[None, :, None, :]).reshape(NODES, NODES)
            )
    return np.stack(result).astype(np.float32)


def matern(dist_sq):
    safe = jnp.maximum(dist_sq, 1e-30)
    scaled = safe * lax.rsqrt(safe)
    decay = jnp.exp(-scaled)
    square = decay * decay
    fourth = square * square
    short = fourth * fourth * fourth
    return decay * (AMPLITUDE + AMPLITUDE * scaled) + short * (
        SHORT_AMPLITUDE + (RATIO * SHORT_AMPLITUDE) * scaled
    )


def split(value):
    high = value.astype(jnp.bfloat16)
    return high, (value - high.astype(jnp.float32)).astype(jnp.bfloat16)


def dot(a, b):
    return jnp.dot(a, b, preferred_element_type=jnp.float32)


def split_dot(a, b):
    a_high, a_low = split(a)
    b_high, b_low = split(b)
    return dot(a_high, b_high) + dot(a_high, b_low) + dot(a_low, b_high)


def leaf_weights(coords, table_ref):
    axes = []
    for axis in range(2):
        t = 2.0 * coords[axis : axis + 1] - 1.0
        terms = [jnp.ones_like(t), t]
        while len(terms) < ORDER:
            terms.append(2.0 * t * terms[-1] - terms[-2])
        total = table_ref[:, 0:1] * terms[0]
        for n in range(1, ORDER):
            total = total + table_ref[:, n : n + 1] * terms[n]
        axes.append(total)
    return jnp.concatenate([axes[0][m : m + 1] * axes[1] for m in range(ORDER)], axis=0)


def up_kernel(side, count_ref, table_ref, maps_ref, offsets_ref, probes_ref, record_ref, *level_refs):
    slots = offsets_ref.shape[2]
    probes = probes_ref.shape[0]
    lane = lax.broadcasted_iota(jnp.int32, (1, slots), 1)
    for leaf in range(side * side):
        count = count_ref[leaf]
        masked = jnp.where(lane < count, probes_ref[:, leaf, :], 0.0)
        coords = offsets_ref[:, leaf, :]
        record_ref[leaf, 0:probes, :] = masked
        record_ref[leaf, probes : probes + 2, :] = coords
        record_ref[leaf, probes + 2 : ROWS, :] = jnp.full(
            (ROWS - probes - 2, slots), count.astype(jnp.float32)
        )
        weights = leaf_weights(coords, table_ref)
        level_refs[0][leaf] = lax.dot_general(
            masked, weights, (((1,), (1,)), ((), ())), precision=HIGHEST,
            preferred_element_type=jnp.float32,
        )
    for level in range(1, len(level_refs)):
        boxes = side >> level
        for x in range(boxes):
            for y in range(boxes):
                total = None
                for child in range(4):
                    source = (2 * x + child // 2) * 2 * boxes + 2 * y + child % 2
                    term = jnp.dot(
                        level_refs[level - 1][source], maps_ref[child], precision=HIGHEST,
                        preferred_element_type=jnp.float32,
                    )
                    total = term if total is None else total + term
                level_refs[level][x * boxes + y] = total


def near_kernel(
    side, count_ref, table_ref, window_ref, local_ref, out_ref, column_ref, probe_ref, result_ref
):
    wide = side + 2
    slots = window_ref.shape[2]
    probes = out_ref.shape[0]
    lane = lax.broadcasted_iota(jnp.int32, (1, slots), 1)

    def prepare(cell, carry):
        column_ref[cell] = jnp.transpose(window_ref[cell, probes:ROWS, :]) * UNIT
        high, low = split(window_ref[cell, 0:probes, :])
        probe_ref[cell] = jnp.concatenate([high, low], axis=0)
        return carry

    lax.fori_loop(0, wide * wide, prepare, 0)

    def one_leaf(leaf, carry):
        i = leaf // side
        j = leaf % side
        center = (i + 1) * wide + j + 1
        coords = window_ref[center, probes : probes + 2, :]
        far = jnp.dot(
            local_ref[leaf], leaf_weights(coords, table_ref), precision=HIGHEST,
            preferred_element_type=jnp.float32,
        )
        scaled_x = coords[0:1] * UNIT
        scaled_y = coords[1:2] * UNIT

        def one_neighbour(n, total):
            a = n // 3
            b = n % 3
            cell = (i + a) * wide + j + b
            row_x = scaled_x - (a - 1).astype(jnp.float32) * UNIT
            row_y = scaled_y - (b - 1).astype(jnp.float32) * UNIT

            def rows(first, size):
                delta_x = row_x - column_ref[cell, first : first + size, 0:1]
                delta_y = row_y - column_ref[cell, first : first + size, 1:2]
                high, low = split(matern(delta_x * delta_x + delta_y * delta_y))
                both = dot(probe_ref[cell, :, first : first + size], high)
                return both[:probes] + both[probes:] + dot(
                    probe_ref[cell, :probes, first : first + size], low
                )

            return lax.cond(
                count_ref[cell] > slots // 2,
                lambda: total + rows(0, slots),
                lambda: lax.cond(
                    count_ref[cell] > 0, lambda: total + rows(0, slots // 2), lambda: total
                ),
            )

        near = lax.fori_loop(0, 9, one_neighbour, jnp.zeros((probes, slots), jnp.float32))
        value = near + far + NUGGET * window_ref[center, 0:probes, :]
        result_ref[leaf] = jnp.where(lane < count_ref[center], value, 0.0)
        return carry

    lax.fori_loop(0, side * side, one_leaf, 0)
    for leaf in range(side * side):
        out_ref[:, leaf, :] = result_ref[leaf]


def list_tables():
    nodes = node_table() / 2.0
    node_x = np.repeat(nodes, ORDER)
    node_y = np.tile(nodes, ORDER)
    source = np.zeros((6, 6, NODES, 8))
    for x in range(6):
        for y in range(6):
            source[x, y, :, 0] = x + node_x
            source[x, y, :, 1] = y + node_y
            source[x, y, :, 2] = x
            source[x, y, :, 3] = y
    target = np.zeros((8, 2, 2, NODES))
    for x in range(2):
        for y in range(2):
            target[0, x, y] = 2 + x + node_x
            target[1, x, y] = 2 + y + node_y
            target[2, x, y] = 2 + x
            target[3, x, y] = 2 + y
    return (
        source.reshape(36 * NODES, 8).astype(np.float32),
        target.reshape(8, 4 * NODES).astype(np.float32),
    )


def list_kernel(source_ref, target_ref, *refs):
    count = len(refs) // 2
    width = target_ref.shape[1]
    for level in range(count):
        scale = UNIT * 2.0**level
        sources_ref, out_ref = refs[level], refs[count + level]
        total = jnp.zeros(out_ref.shape, jnp.float32)
        for group in range(source_ref.shape[0] // width):
            rows = slice(group * width, (group + 1) * width)
            delta_x = (target_ref[0:1] - source_ref[rows, 0:1]) * scale
            delta_y = (target_ref[1:2] - source_ref[rows, 1:2]) * scale
            apart = jnp.maximum(
                jnp.abs(target_ref[2:3] - source_ref[rows, 2:3]),
                jnp.abs(target_ref[3:4] - source_ref[rows, 3:4]),
            )
            matrix = jnp.where(apart > 1.5, matern(delta_x * delta_x + delta_y * delta_y), 0.0)
            total = total + split_dot(sources_ref[:, rows], matrix)
        out_ref[...] = total


def extended(block, sides, width):
    for axis, dim in sides:
        count = lax.axis_size(axis)
        forward = [(i, i + 1) for i in range(count - 1)]
        backward = [(target, source) for source, target in forward]
        low = lax.ppermute(
            lax.slice_in_dim(block, block.shape[dim] - width, None, axis=dim), axis, forward
        )
        high = lax.ppermute(lax.slice_in_dim(block, 0, width, axis=dim), axis, backward)
        block = jnp.concatenate([low, block, high], axis=dim)
    return block


def upward(children, maps):
    half_x = children.shape[0] // 2
    half_y = children.shape[1] // 2
    grouped = children.reshape((half_x, 2, half_y, 2) + children.shape[2:])
    return jnp.einsum(
        "xyrq,ixjypr->ijpq", maps.reshape(2, 2, NODES, NODES), grouped, precision=HIGHEST
    )


def interact_top(box_grid, own_x, own_y, box_side):
    nodes = jnp.asarray(node_table() * (box_side / 2.0), jnp.float32)
    node_x = jnp.repeat(nodes, ORDER)
    node_y = jnp.tile(nodes, ORDER)
    shift_x = (jnp.arange(box_grid.shape[0], dtype=jnp.int32) - own_x).astype(jnp.float32)
    shift_y = (jnp.arange(box_grid.shape[1], dtype=jnp.int32) - own_y).astype(jnp.float32)
    delta_x = (node_x[:, None] - node_x[None, :] - shift_x[:, None, None] * box_side) * UNIT
    delta_y = (node_y[:, None] - node_y[None, :] - shift_y[:, None, None] * box_side) * UNIT
    matrices = matern((delta_x * delta_x)[:, None] + (delta_y * delta_y)[None])
    separated = jnp.maximum(jnp.abs(shift_x)[:, None], jnp.abs(shift_y)[None]) >= 2.0
    return jnp.einsum(
        "abqr,abpr->pq",
        jnp.where(separated[:, :, None, None], matrices, 0.0),
        box_grid,
        precision=HIGHEST,
    )


def flat_list(window):
    return jnp.transpose(window, (2, 0, 1, 3)).reshape(window.shape[2], -1)


def per_device(offsets, probes, counts):
    count_p, side, _, slots = probes.shape
    depth = side.bit_length() - 1
    top = depth + 2
    index_x = lax.axis_index("gx")
    index_y = lax.axis_index("gy")
    size_x = lax.axis_size("gx")
    size_y = lax.axis_size("gy")
    leaves = side * side
    table = jnp.asarray(series_at_nodes().T, jnp.float32)
    maps = jnp.asarray(child_maps())
    smem = pl.BlockSpec(memory_space=pltpu.SMEM)
    vmem = pl.BlockSpec(memory_space=pltpu.VMEM)
    levels = pl.pallas_call(
        functools.partial(up_kernel, side),
        out_shape=[jax.ShapeDtypeStruct((leaves, ROWS, slots), jnp.float32)]
        + [
            jax.ShapeDtypeStruct(((side >> level) ** 2, count_p, NODES), jnp.float32)
            for level in range(depth + 1)
        ],
        in_specs=[smem, vmem, vmem, vmem, vmem],
        out_specs=[vmem] * (depth + 2),
        name="up",
    )(
        counts.reshape(leaves),
        table,
        maps,
        offsets.reshape(2, leaves, slots),
        probes.reshape(count_p, leaves, slots),
    )
    record, levels = levels[0], levels[1:]
    window = extended(record.reshape(side, side, ROWS, slots), (("gx", 0), ("gy", 1)), 1)
    wide = side + 2
    window_counts = window[:, :, count_p + 2, 0].astype(jnp.int32).reshape(wide * wide)

    lists = []
    for level in range(depth):
        boxes = side >> level
        flat = levels[level].reshape(boxes, boxes, count_p * NODES)
        rim = extended(flat, (("gx", 0), ("gy", 1)), 2)
        rim = rim.reshape(boxes + 4, boxes + 4, count_p, NODES)
        lists.append(
            jnp.concatenate(
                [
                    flat_list(rim[2 * x : 2 * x + 6, 2 * y : 2 * y + 6])
                    for x in range(boxes // 2)
                    for y in range(boxes // 2)
                ],
                axis=0,
            )
        )
    gathered = lax.all_gather(
        levels[depth].reshape(1, count_p * NODES), ("gx", "gy"), axis=0, tiled=True
    )
    grids = [gathered.reshape(size_x, size_y, count_p, NODES)]
    for _ in range(top - depth):
        grids.append(upward(grids[-1], maps))
    for level in range(depth, top):
        shrink = 2 ** (level - depth)
        padded = jnp.pad(grids[level - depth], ((2, 2), (2, 2), (0, 0), (0, 0)))
        first_x = index_x // (2 * shrink) * 2
        first_y = index_y // (2 * shrink) * 2
        lists.append(
            flat_list(
                lax.dynamic_slice(padded, (first_x, first_y, 0, 0), (6, 6, count_p, NODES))
            )
        )
    source_table, target_table = list_tables()
    met = pl.pallas_call(
        list_kernel,
        out_shape=[
            jax.ShapeDtypeStruct((entry.shape[0], 4 * NODES), jnp.float32) for entry in lists
        ],
        in_specs=[vmem] * (2 + len(lists)),
        out_specs=[vmem] * len(lists),
        name="lists",
    )(jnp.asarray(source_table), jnp.asarray(target_table), *lists)

    if max(grids[-1].shape[:2]) > 2:
        local = interact_top(grids[-1], index_x // 2**(top - depth), index_y // 2**(top - depth), 2.0**top)
    else:
        local = jnp.zeros((count_p, NODES), jnp.float32)
    for level in range(top - 1, depth - 1, -1):
        shrink = 2 ** (level - depth)
        child = (index_x // shrink) % 2 * 2 + (index_y // shrink) % 2
        own_map = lax.dynamic_index_in_dim(maps, child, 0, keepdims=False)
        own = lax.dynamic_slice_in_dim(met[level], child * NODES, NODES, axis=1)
        local = own + jnp.einsum("rq,pq->pr", own_map, local, precision=HIGHEST)
    local = local[None, None]
    for level in range(depth - 1, -1, -1):
        half = local.shape[0]
        spread = jnp.einsum("crq,ijpq->ijpcr", maps, local, precision=HIGHEST)
        spread = spread + met[level].reshape(half, half, count_p, 4, NODES)
        spread = spread.reshape(half, half, count_p, 2, 2, NODES)
        local = jnp.transpose(spread, (0, 3, 1, 4, 2, 5)).reshape(
            2 * half, 2 * half, count_p, NODES
        )
    result = pl.pallas_call(
        functools.partial(near_kernel, side),
        out_shape=jax.ShapeDtypeStruct((count_p, leaves, slots), jnp.float32),
        in_specs=[smem, vmem, vmem, vmem],
        out_specs=vmem,
        scratch_shapes=[
            pltpu.VMEM((wide * wide, slots, 8), jnp.float32),
            pltpu.VMEM((wide * wide, 2 * count_p, slots), jnp.bfloat16),
            pltpu.VMEM((leaves, count_p, slots), jnp.float32),
        ],
        name="near",
    )(
        window_counts,
        table,
        window.reshape(wide * wide, ROWS, slots),
        local.reshape(leaves, count_p, NODES),
    )
    return result.reshape(count_p, side, side, slots)


def solution(mesh):
    placed = (P(None, "gx", "gy", None), P(None, "gx", "gy", None), P("gx", "gy"))
    return jax.shard_map(
        per_device, mesh=mesh, in_specs=placed, out_specs=P(None, "gx", "gy", None), check_vma=False
    )
```

```python
import functools
import math

import jax
import jax.numpy as jnp
import numpy as np
from jax import lax
from jax.experimental import pallas as pl
from jax.experimental.pallas import tpu as pltpu
from jax.sharding import PartitionSpec as P

ORDER = 8
NODES = ORDER * ORDER
ROOT_THREE = 1.7320508075688772
LENGTH_SCALE = 6.0
AMPLITUDE = 1.0 / 96.0
SHORT_AMPLITUDE = 1.0 / 16.0
NUGGET = 0.5
RATIO = 12
UNIT = ROOT_THREE / LENGTH_SCALE
HIGH = lax.Precision.HIGH
HIGHEST = lax.Precision.HIGHEST
ROWS = 24


def node_table():
    slots = np.arange(ORDER)
    return np.cos((2.0 * slots + 1.0) * (np.pi / (2.0 * ORDER)))


def series_at_nodes():
    powers = np.arange(ORDER)
    slots = np.arange(ORDER)
    table = np.cos(powers[:, None] * (2.0 * slots[None, :] + 1.0) * (np.pi / (2.0 * ORDER)))
    table = table * (2.0 / ORDER)
    table[0] = 1.0 / ORDER
    return table


def interpolation(coords):
    angles = np.arccos(np.clip(coords, -1.0, 1.0))
    series = np.cos(angles[:, None] * np.arange(ORDER))
    return series @ series_at_nodes()


def child_maps():
    nodes = node_table()
    result = []
    for child_x in range(2):
        for child_y in range(2):
            weight_x = interpolation((nodes - 1.0) / 2.0 + child_x)
            weight_y = interpolation((nodes - 1.0) / 2.0 + child_y)
            result.append(
                (weight_x[:, None, :, None] * weight_y[None, :, None, :]).reshape(NODES, NODES)
            )
    return np.stack(result).astype(np.float32)


def matern(dist_sq):
    safe = jnp.maximum(dist_sq, 1e-30)
    scaled = safe * lax.rsqrt(safe)
    decay = jnp.exp(-scaled)
    square = decay * decay
    fourth = square * square
    short = fourth * fourth * fourth
    return decay * (AMPLITUDE + AMPLITUDE * scaled) + short * (
        SHORT_AMPLITUDE + (RATIO * SHORT_AMPLITUDE) * scaled
    )


def split(value):
    high = value.astype(jnp.bfloat16)
    return high, (value - high.astype(jnp.float32)).astype(jnp.bfloat16)


def dot(a, b):
    return jnp.dot(a, b, preferred_element_type=jnp.float32)


def split_dot(a, b):
    a_high, a_low = split(a)
    b_high, b_low = split(b)
    return dot(a_high, b_high) + dot(a_high, b_low) + dot(a_low, b_high)


def leaf_weights(coords, table_ref):
    axes = []
    for axis in range(2):
        t = 2.0 * coords[axis : axis + 1] - 1.0
        terms = [jnp.ones_like(t), t]
        while len(terms) < ORDER:
            terms.append(2.0 * t * terms[-1] - terms[-2])
        total = table_ref[:, 0:1] * terms[0]
        for n in range(1, ORDER):
            total = total + table_ref[:, n : n + 1] * terms[n]
        axes.append(total)
    return jnp.concatenate([axes[0][m : m + 1] * axes[1] for m in range(ORDER)], axis=0)


def up_kernel(side, count_ref, table_ref, maps_ref, offsets_ref, probes_ref, record_ref, *level_refs):
    slots = offsets_ref.shape[3]
    probes = probes_ref.shape[0]
    lane = lax.broadcasted_iota(jnp.int32, (1, slots), 1)
    for i in range(side):
        for j in range(side):
            count = count_ref[i, j]
            masked = jnp.where(lane < count, probes_ref[:, i, j, :], 0.0)
            coords = offsets_ref[:, i, j, :]
            record_ref[i, j, 0:probes, :] = masked
            record_ref[i, j, probes : probes + 2, :] = coords
            record_ref[i, j, probes + 2 : ROWS, :] = jnp.full(
                (ROWS - probes - 2, slots), count.astype(jnp.float32)
            )
            level_refs[0][i, j] = dot_rows(masked, leaf_weights(coords, table_ref))
    for level in range(1, len(level_refs)):
        boxes = side >> level
        for x in range(boxes):
            for y in range(boxes):
                level_refs[level][x, y] = merged(level_refs[level - 1], x, y, maps_ref)


def dot_rows(a, b):
    return lax.dot_general(
        a, b, (((1,), (1,)), ((), ())), precision=HIGHEST, preferred_element_type=jnp.float32
    )


def merged(children_ref, x, y, maps_ref, pad=0):
    total = None
    for child in range(4):
        term = jnp.dot(
            children_ref[pad + 2 * x + child // 2, pad + 2 * y + child % 2],
            maps_ref[child],
            precision=HIGHEST,
            preferred_element_type=jnp.float32,
        )
        total = term if total is None else total + term
    return total


def exchange_kernel(sizes, *refs):
    size_x, size_y = sizes
    sources, own_ref = refs[0:3], refs[3]
    windows, grid_ref = refs[4:7], refs[7]
    send_sem, recv_sem, line_send, line_recv, own_sem = refs[8:]
    ix = lax.axis_index("gx")
    iy = lax.axis_index("gy")
    steps = [(dx, dy) for dx in (-1, 0, 1) for dy in (-1, 0, 1) if (dx, dy) != (0, 0)]

    def inside(dx, dy):
        x = ix + dx
        y = iy + dy
        return (x >= 0) & (x < size_x) & (y >= 0) & (y < size_y)

    own_copy = pltpu.make_async_copy(own_ref.at[0, 0], grid_ref.at[ix, iy], own_sem)
    own_copy.start()
    for source, window in zip(sources, windows):
        side = source.shape[0]
        width = (window.shape[0] - side) // 2
        window[...] = jnp.zeros_like(window)
        window[width : width + side, width : width + side] = source[...]

    barrier = pltpu.get_barrier_semaphore()

    def greet(x, y):
        pl.semaphore_signal(
            barrier, inc=1, device_id=(x, y), device_id_type=pl.DeviceIdType.MESH
        )

    for k in range(1, size_x):
        greet(lax.rem(ix + k, size_x), iy)
    for k in range(1, size_y):
        greet(ix, lax.rem(iy + k, size_y))
    for dx, dy in steps:
        if dx and dy:
            pl.when(inside(dx, dy))(lambda dx=dx, dy=dy: greet(ix + dx, iy + dy))
    sides_x = jnp.minimum(ix, 1) + jnp.minimum(size_x - 1 - ix, 1)
    sides_y = jnp.minimum(iy, 1) + jnp.minimum(size_y - 1 - iy, 1)
    pl.semaphore_wait(barrier, size_x + size_y - 2 + sides_x * sides_y)

    def line_copy(slot, source, target, x, y):
        return pltpu.make_async_remote_copy(
            src_ref=source,
            dst_ref=target,
            send_sem=line_send.at[slot],
            recv_sem=line_recv.at[slot],
            device_id=(x, y),
            device_id_type=pl.DeviceIdType.MESH,
        )

    along_x = [
        line_copy(k - 1, own_ref.at[0, 0], grid_ref.at[ix, iy], lax.rem(ix + k, size_x), iy)
        for k in range(1, size_x)
    ]
    for copy in along_x:
        copy.start()

    def pieces(step, side, width):
        if step > 0:
            return pl.ds(side - width, width), pl.ds(0, width)
        if step < 0:
            return pl.ds(0, width), pl.ds(side + width, width)
        return pl.ds(0, side), pl.ds(width, side)

    def halo_copy(n, which):
        dx, dy = steps[n]
        source, window = sources[which], windows[which]
        side = source.shape[0]
        width = (window.shape[0] - side) // 2
        from_x, to_x = pieces(dx, side, width)
        from_y, to_y = pieces(dy, side, width)
        return pltpu.make_async_remote_copy(
            src_ref=source.at[from_x, from_y],
            dst_ref=window.at[to_x, to_y],
            send_sem=send_sem.at[which, n],
            recv_sem=recv_sem.at[which, n],
            device_id=(ix + dx, iy + dy),
            device_id_type=pl.DeviceIdType.MESH,
        )

    order = [(which, n) for which in range(3) for n in range(len(steps))]
    for which, n in order:
        pl.when(inside(*steps[n]))(lambda which=which, n=n: halo_copy(n, which).start())
    for copy in along_x:
        copy.wait_recv()
    own_copy.wait()
    along_y = [
        line_copy(
            size_x - 1 + k - 1, grid_ref.at[:, iy], grid_ref.at[:, iy],
            ix, lax.rem(iy + k, size_y),
        )
        for k in range(1, size_y)
    ]
    for copy in along_y:
        copy.start()
    for which, n in order:
        dx, dy = steps[n]
        pl.when(inside(-dx, -dy))(lambda which=which, n=n: halo_copy(n, which).wait_recv())
    for copy in along_y:
        copy.wait_recv()
    for which, n in order:
        pl.when(inside(*steps[n]))(lambda which=which, n=n: halo_copy(n, which).wait_send())
    for copy in along_x + along_y:
        copy.wait_send()


def near_kernel(
    side, count_ref, table_ref, window_ref, local_ref, out_ref, column_ref, probe_ref, result_ref
):
    wide = side + 2
    slots = window_ref.shape[3]
    probes = out_ref.shape[0]
    lane = lax.broadcasted_iota(jnp.int32, (1, slots), 1)

    def prepare(cell, carry):
        x = cell // wide
        y = cell % wide
        column_ref[cell] = jnp.transpose(window_ref[x, y, probes:ROWS, :]) * UNIT
        high, low = split(window_ref[x, y, 0:probes, :])
        probe_ref[cell] = jnp.concatenate([high, low], axis=0)
        return carry

    lax.fori_loop(0, wide * wide, prepare, 0)

    def one_leaf(leaf, carry):
        i = leaf // side
        j = leaf % side
        center = (i + 1) * wide + j + 1
        coords = window_ref[i + 1, j + 1, probes : probes + 2, :]
        far = jnp.dot(
            local_ref[i, j], leaf_weights(coords, table_ref), precision=HIGHEST,
            preferred_element_type=jnp.float32,
        )
        scaled_x = coords[0:1] * UNIT
        scaled_y = coords[1:2] * UNIT

        def one_neighbour(n, total):
            a = n // 3
            b = n % 3
            cell = (i + a) * wide + j + b
            row_x = scaled_x - (a - 1).astype(jnp.float32) * UNIT
            row_y = scaled_y - (b - 1).astype(jnp.float32) * UNIT

            def rows(first, size):
                delta_x = row_x - column_ref[cell, first : first + size, 0:1]
                delta_y = row_y - column_ref[cell, first : first + size, 1:2]
                high, low = split(matern(delta_x * delta_x + delta_y * delta_y))
                both = dot(probe_ref[cell, :, first : first + size], high)
                return both[:probes] + both[probes:] + dot(
                    probe_ref[cell, :probes, first : first + size], low
                )

            return lax.cond(
                count_ref[cell] > slots // 2,
                lambda: total + rows(0, slots),
                lambda: lax.cond(
                    count_ref[cell] > 0, lambda: total + rows(0, slots // 2), lambda: total
                ),
            )

        near = lax.fori_loop(0, 9, one_neighbour, jnp.zeros((probes, slots), jnp.float32))
        value = near + far + NUGGET * window_ref[i + 1, j + 1, 0:probes, :]
        result_ref[leaf] = jnp.where(lane < count_ref[center], value, 0.0)
        return carry

    lax.fori_loop(0, side * side, one_leaf, 0)
    for leaf in range(side * side):
        out_ref[:, leaf // side, leaf % side, :] = result_ref[leaf]


def list_tables():
    nodes = node_table() / 2.0
    node_x = np.repeat(nodes, ORDER)
    node_y = np.tile(nodes, ORDER)
    source = np.zeros((6, 6, NODES, 8))
    for x in range(6):
        for y in range(6):
            source[x, y, :, 0] = x + node_x
            source[x, y, :, 1] = y + node_y
            source[x, y, :, 2] = x
            source[x, y, :, 3] = y
    target = np.zeros((8, 2, 2, NODES))
    for x in range(2):
        for y in range(2):
            target[0, x, y] = 2 + x + node_x
            target[1, x, y] = 2 + y + node_y
            target[2, x, y] = 2 + x
            target[3, x, y] = 2 + y
    return (
        source.reshape(36 * NODES, 8).astype(np.float32),
        target.reshape(8, 4 * NODES).astype(np.float32),
    )


def matrices(target_ref, source_ref, rows, lanes, scale):
    delta_x = (target_ref[0:1, lanes] - source_ref[rows, 0:1]) * scale
    delta_y = (target_ref[1:2, lanes] - source_ref[rows, 1:2]) * scale
    apart = jnp.maximum(
        jnp.abs(target_ref[2:3, lanes] - source_ref[rows, 2:3]),
        jnp.abs(target_ref[3:4, lanes] - source_ref[rows, 3:4]),
    )
    return jnp.where(apart > 1.5, matern(delta_x * delta_x + delta_y * delta_y), 0.0)


def list_kernel(
    depth, extra, position_ref, source_ref, target_ref, far_target_ref, maps_ref, top_ref, *refs
):
    rims, grid_ref, out_ref = refs[:depth], refs[depth], refs[depth + 1]
    padded = refs[depth + 2 : depth + 2 + extra]
    locals_ref = refs[depth + 2 + extra :]
    probes = top_ref.shape[0]
    width = target_ref.shape[1]
    groups = source_ref.shape[0] // width
    per_group = width // NODES

    for level in range(extra):
        padded[level][...] = jnp.zeros_like(padded[level])
        count_x = padded[level].shape[0] - 4
        count_y = padded[level].shape[1] - 4
        if level == 0:
            padded[0][2 : 2 + count_x, 2 : 2 + count_y] = grid_ref[...]
        else:
            for x in range(count_x):
                for y in range(count_y):
                    padded[level][2 + x, 2 + y] = merged(padded[level - 1], x, y, maps_ref, 2)

    def gathered(load, group):
        boxes = [group * per_group + n for n in range(per_group)]
        return jnp.concatenate([load(box // 6, box % 6) for box in boxes], axis=1)

    ix = position_ref[0]
    iy = position_ref[1]
    own_child = []
    for level in range(extra):
        own_child.append((ix >> level) % 2 * 2 + (iy >> level) % 2)
    lanes = slice(0, extra * NODES)
    scales = far_target_ref[4:5, lanes]
    total = jnp.zeros((extra * probes, extra * NODES), jnp.float32)
    for group in range(groups):
        parts = []
        for level in range(extra):
            first_x = (ix >> (level + 1)) * 2
            first_y = (iy >> (level + 1)) * 2
            parts.append(
                gathered(lambda x, y: padded[level][first_x + x, first_y + y], group)
            )
        rows = slice(group * width, (group + 1) * width)
        matrix = matrices(far_target_ref, source_ref, rows, lanes, scales)
        total = total + split_dot(jnp.concatenate(parts, axis=0), matrix)
    local = top_ref[...]
    for level in range(extra - 1, -1, -1):
        own = total[level * probes : (level + 1) * probes, level * NODES : (level + 1) * NODES]
        local = own + dot_rows(local, maps_ref[own_child[level]])
    locals_ref[depth][0, 0] = local

    for level in range(depth - 1, -1, -1):
        rim_ref = rims[level]
        half = (rim_ref.shape[0] - 4) // 2
        total = jnp.zeros((half * half * probes, width), jnp.float32)
        for group in range(groups):
            parts = [
                gathered(lambda x, y: rim_ref[2 * px + x, 2 * py + y], group)
                for px in range(half)
                for py in range(half)
            ]
            rows = slice(group * width, (group + 1) * width)
            matrix = matrices(
                target_ref, source_ref, rows, slice(0, width), UNIT * 2.0**level
            )
            total = total + split_dot(jnp.concatenate(parts, axis=0), matrix)
        target = out_ref if level == 0 else locals_ref[level]
        above = jnp.concatenate(
            [locals_ref[level + 1][px, py] for px in range(half) for py in range(half)], axis=0
        )
        for child in range(4):
            value = total[:, child * NODES : (child + 1) * NODES] + dot_rows(
                above, maps_ref[child]
            )
            for box in range(half * half):
                target[2 * (box // half) + child // 2, 2 * (box % half) + child % 2] = value[
                    box * probes : (box + 1) * probes
                ]


def upward(children, maps):
    half_x = children.shape[0] // 2
    half_y = children.shape[1] // 2
    grouped = children.reshape((half_x, 2, half_y, 2) + children.shape[2:])
    return jnp.einsum(
        "xyrq,ixjypr->ijpq", maps.reshape(2, 2, NODES, NODES), grouped, precision=HIGHEST
    )


def interact_top(box_grid, own_x, own_y, box_side):
    nodes = jnp.asarray(node_table() * (box_side / 2.0), jnp.float32)
    node_x = jnp.repeat(nodes, ORDER)
    node_y = jnp.tile(nodes, ORDER)
    shift_x = (jnp.arange(box_grid.shape[0], dtype=jnp.int32) - own_x).astype(jnp.float32)
    shift_y = (jnp.arange(box_grid.shape[1], dtype=jnp.int32) - own_y).astype(jnp.float32)
    delta_x = (node_x[:, None] - node_x[None, :] - shift_x[:, None, None] * box_side) * UNIT
    delta_y = (node_y[:, None] - node_y[None, :] - shift_y[:, None, None] * box_side) * UNIT
    matrices = matern((delta_x * delta_x)[:, None] + (delta_y * delta_y)[None])
    separated = jnp.maximum(jnp.abs(shift_x)[:, None], jnp.abs(shift_y)[None]) >= 2.0
    return jnp.einsum(
        "abqr,abpr->pq",
        jnp.where(separated[:, :, None, None], matrices, 0.0),
        box_grid,
        precision=HIGHEST,
    )


def per_device(offsets, probes, counts):
    count_p, side, _, slots = probes.shape
    depth = side.bit_length() - 1
    extra = 2
    top = depth + extra
    index_x = lax.axis_index("gx")
    index_y = lax.axis_index("gy")
    size_x = lax.axis_size("gx")
    size_y = lax.axis_size("gy")
    wide = side + 2
    table = jnp.asarray(series_at_nodes().T, jnp.float32)
    maps = jnp.asarray(child_maps())
    smem = pl.BlockSpec(memory_space=pltpu.SMEM)
    vmem = pl.BlockSpec(memory_space=pltpu.VMEM)

    def shape(*dims):
        return jax.ShapeDtypeStruct(dims, jnp.float32)

    record, *levels = pl.pallas_call(
        functools.partial(up_kernel, side),
        out_shape=[shape(side, side, ROWS, slots)]
        + [shape(side >> k, side >> k, count_p, NODES) for k in range(depth + 1)],
        in_specs=[smem, vmem, vmem, vmem, vmem],
        out_specs=[vmem] * (depth + 2),
        name="up",
    )(counts, table, maps, offsets, probes)
    window, *rims, grid = pl.pallas_call(
        functools.partial(exchange_kernel, (size_x, size_y)),
        out_shape=[shape(wide, wide, ROWS, slots)]
        + [shape((side >> k) + 4, (side >> k) + 4, count_p, NODES) for k in range(depth)]
        + [shape(size_x, size_y, count_p, NODES)],
        in_specs=[vmem] * (depth + 2),
        out_specs=[vmem] * (depth + 2),
        scratch_shapes=[
            pltpu.SemaphoreType.DMA((depth + 1, 8)),
            pltpu.SemaphoreType.DMA((depth + 1, 8)),
            pltpu.SemaphoreType.DMA((size_x + size_y - 2,)),
            pltpu.SemaphoreType.DMA((size_x + size_y - 2,)),
            pltpu.SemaphoreType.DMA,
        ],
        compiler_params=pltpu.CompilerParams(collective_id=0, has_side_effects=True),
        name="exchange",
    )(record, *levels)

    if max(size_x, size_y) > 2 * 2**extra:
        grids = [grid]
        for _ in range(extra):
            grids.append(upward(grids[-1], maps))
        local = interact_top(grids[-1], index_x // 2**extra, index_y // 2**extra, 2.0**top)
    else:
        local = jnp.zeros((count_p, NODES), jnp.float32)
    source_table, target_table = list_tables()
    target_rows = jnp.asarray(target_table).reshape(8, 4, NODES)
    far_target = []
    for k in range(extra):
        child = (index_x >> k) % 2 * 2 + (index_y >> k) % 2
        rows = lax.dynamic_index_in_dim(target_rows, child, 1, keepdims=False)
        far_target.append(rows.at[4].set(UNIT * 2.0 ** (depth + k)))
    local = pl.pallas_call(
        functools.partial(list_kernel, depth, extra),
        out_shape=shape(side, side, count_p, NODES),
        in_specs=[smem] + [vmem] * (5 + depth + 1),
        out_specs=vmem,
        scratch_shapes=[
            pltpu.VMEM(((size_x >> k) + 4, (size_y >> k) + 4, count_p, NODES), jnp.float32)
            for k in range(extra)
        ]
        + [
            pltpu.VMEM((side >> k, side >> k, count_p, NODES), jnp.float32)
            for k in range(depth + 1)
        ],
        name="lists",
    )(
        jnp.stack([index_x, index_y]).astype(jnp.int32),
        jnp.asarray(source_table),
        jnp.asarray(target_table),
        jnp.concatenate(far_target, axis=1),
        maps,
        local,
        *rims,
        grid,
    )
    return pl.pallas_call(
        functools.partial(near_kernel, side),
        out_shape=shape(count_p, side, side, slots),
        in_specs=[smem, vmem, vmem, vmem],
        out_specs=vmem,
        scratch_shapes=[
            pltpu.VMEM((wide * wide, slots, 8), jnp.float32),
            pltpu.VMEM((wide * wide, 2 * count_p, slots), jnp.bfloat16),
            pltpu.VMEM((side * side, count_p, slots), jnp.float32),
        ],
        name="near",
    )(
        window[:, :, count_p + 2, 0].astype(jnp.int32).reshape(wide * wide),
        table,
        window,
        local,
    )


def solution(mesh):
    placed = (P(None, "gx", "gy", None), P(None, "gx", "gy", None), P("gx", "gy"))
    return jax.shard_map(
        per_device, mesh=mesh, in_specs=placed, out_specs=P(None, "gx", "gy", None), check_vma=False
    )
```

```python
import functools
import math

import jax
import jax.numpy as jnp
import numpy as np
from jax import lax
from jax.experimental import pallas as pl
from jax.experimental.pallas import tpu as pltpu
from jax.sharding import PartitionSpec as P

ORDER = 8
NODES = ORDER * ORDER
ROOT_THREE = 1.7320508075688772
LENGTH_SCALE = 6.0
AMPLITUDE = 1.0 / 96.0
SHORT_AMPLITUDE = 1.0 / 16.0
NUGGET = 0.5
RATIO = 12
UNIT = ROOT_THREE * RATIO / LENGTH_SCALE
FACTOR = AMPLITUDE / RATIO
LOG2_E = 1.4426950408889634
SHORT_SHIFT = math.log2(SHORT_AMPLITUDE / FACTOR)
HIGH = lax.Precision.HIGH
HIGHEST = lax.Precision.HIGHEST
ROWS = 24


def node_table():
    slots = np.arange(ORDER)
    return np.cos((2.0 * slots + 1.0) * (np.pi / (2.0 * ORDER)))


def series_at_nodes():
    powers = np.arange(ORDER)
    slots = np.arange(ORDER)
    table = np.cos(powers[:, None] * (2.0 * slots[None, :] + 1.0) * (np.pi / (2.0 * ORDER)))
    table = table * (2.0 / ORDER)
    table[0] = 1.0 / ORDER
    return table


def interpolation(coords):
    angles = np.arccos(np.clip(coords, -1.0, 1.0))
    series = np.cos(angles[:, None] * np.arange(ORDER))
    return series @ series_at_nodes()


def child_maps():
    nodes = node_table()
    result = []
    for child_x in range(2):
        for child_y in range(2):
            weight_x = interpolation((nodes - 1.0) / 2.0 + child_x)
            weight_y = interpolation((nodes - 1.0) / 2.0 + child_y)
            result.append(
                (weight_x[:, None, :, None] * weight_y[None, :, None, :]).reshape(NODES, NODES)
            )
    return np.stack(result).astype(np.float32)


def matern(dist_sq):
    safe = jnp.maximum(dist_sq, 1e-30)
    scaled = safe * lax.rsqrt(safe)
    decay = jnp.exp2(scaled * (-LOG2_E / RATIO))
    short = jnp.exp2(scaled * -LOG2_E + SHORT_SHIFT)
    return decay * (scaled + RATIO) + short * (scaled + 1.0)


def split(value):
    high = value.astype(jnp.bfloat16)
    return high, (value - high.astype(jnp.float32)).astype(jnp.bfloat16)


def dot(a, b):
    return jnp.dot(a, b, preferred_element_type=jnp.float32)


def split_dot(a, b):
    a_high, a_low = split(a)
    b_high, b_low = split(b)
    return dot(a_high, b_high) + dot(a_high, b_low) + dot(a_low, b_high)


def leaf_weights(coords, table_ref):
    axes = []
    for axis in range(2):
        t = 2.0 * coords[axis : axis + 1] - 1.0
        terms = [jnp.ones_like(t), t]
        while len(terms) < ORDER:
            terms.append(2.0 * t * terms[-1] - terms[-2])
        total = table_ref[:, 0:1] * terms[0]
        for n in range(1, ORDER):
            total = total + table_ref[:, n : n + 1] * terms[n]
        axes.append(total)
    return jnp.concatenate([axes[0][m : m + 1] * axes[1] for m in range(ORDER)], axis=0)


def up_kernel(side, count_ref, table_ref, maps_ref, offsets_ref, probes_ref, record_ref, *level_refs):
    slots = offsets_ref.shape[3]
    probes = probes_ref.shape[0]
    lane = lax.broadcasted_iota(jnp.int32, (1, slots), 1)
    for i in range(side):
        for j in range(side):
            count = count_ref[i, j]
            masked = jnp.where(lane < count, probes_ref[:, i, j, :], 0.0)
            coords = offsets_ref[:, i, j, :]
            record_ref[i, j, 0:probes, :] = masked
            record_ref[i, j, probes : probes + 2, :] = coords
            record_ref[i, j, probes + 2 : ROWS, :] = jnp.full(
                (ROWS - probes - 2, slots), count.astype(jnp.float32)
            )
            level_refs[0][i, j] = dot_rows(masked, leaf_weights(coords, table_ref))
    for level in range(1, len(level_refs)):
        boxes = side >> level
        for x in range(boxes):
            for y in range(boxes):
                level_refs[level][x, y] = merged(level_refs[level - 1], x, y, maps_ref)


def dot_rows(a, b):
    return lax.dot_general(
        a, b, (((1,), (1,)), ((), ())), precision=HIGHEST, preferred_element_type=jnp.float32
    )


def merged(children_ref, x, y, maps_ref, pad=0):
    total = None
    for child in range(4):
        term = jnp.dot(
            children_ref[pad + 2 * x + child // 2, pad + 2 * y + child % 2],
            maps_ref[child],
            precision=HIGHEST,
            preferred_element_type=jnp.float32,
        )
        total = term if total is None else total + term
    return total


def exchange_kernel(sizes, *refs):
    size_x, size_y = sizes
    sources, own_ref = refs[0:3], refs[3]
    windows, grid_ref = refs[4:7], refs[7]
    send_sem, recv_sem, line_send, line_recv, own_sem = refs[8:]
    ix = lax.axis_index("gx")
    iy = lax.axis_index("gy")
    steps = [(dx, dy) for dx in (-1, 0, 1) for dy in (-1, 0, 1) if (dx, dy) != (0, 0)]

    def inside(dx, dy):
        x = ix + dx
        y = iy + dy
        return (x >= 0) & (x < size_x) & (y >= 0) & (y < size_y)

    own_copy = pltpu.make_async_copy(own_ref.at[0, 0], grid_ref.at[ix, iy], own_sem)
    own_copy.start()
    for source, window in zip(sources, windows):
        side = source.shape[0]
        width = (window.shape[0] - side) // 2
        window[...] = jnp.zeros_like(window)
        window[width : width + side, width : width + side] = source[...]

    barrier = pltpu.get_barrier_semaphore()

    def greet(x, y):
        pl.semaphore_signal(
            barrier, inc=1, device_id=(x, y), device_id_type=pl.DeviceIdType.MESH
        )

    for k in range(1, size_x):
        greet(lax.rem(ix + k, size_x), iy)
    for k in range(1, size_y):
        greet(ix, lax.rem(iy + k, size_y))
    for dx, dy in steps:
        if dx and dy:
            pl.when(inside(dx, dy))(lambda dx=dx, dy=dy: greet(ix + dx, iy + dy))
    sides_x = jnp.minimum(ix, 1) + jnp.minimum(size_x - 1 - ix, 1)
    sides_y = jnp.minimum(iy, 1) + jnp.minimum(size_y - 1 - iy, 1)
    pl.semaphore_wait(barrier, size_x + size_y - 2 + sides_x * sides_y)

    def line_copy(slot, source, target, x, y):
        return pltpu.make_async_remote_copy(
            src_ref=source,
            dst_ref=target,
            send_sem=line_send.at[slot],
            recv_sem=line_recv.at[slot],
            device_id=(x, y),
            device_id_type=pl.DeviceIdType.MESH,
        )

    along_x = [
        line_copy(k - 1, own_ref.at[0, 0], grid_ref.at[ix, iy], lax.rem(ix + k, size_x), iy)
        for k in range(1, size_x)
    ]
    for copy in along_x:
        copy.start()

    def pieces(step, side, width):
        if step > 0:
            return pl.ds(side - width, width), pl.ds(0, width)
        if step < 0:
            return pl.ds(0, width), pl.ds(side + width, width)
        return pl.ds(0, side), pl.ds(width, side)

    def halo_copy(n, which):
        dx, dy = steps[n]
        source, window = sources[which], windows[which]
        side = source.shape[0]
        width = (window.shape[0] - side) // 2
        from_x, to_x = pieces(dx, side, width)
        from_y, to_y = pieces(dy, side, width)
        return pltpu.make_async_remote_copy(
            src_ref=source.at[from_x, from_y],
            dst_ref=window.at[to_x, to_y],
            send_sem=send_sem.at[which, n],
            recv_sem=recv_sem.at[which, n],
            device_id=(ix + dx, iy + dy),
            device_id_type=pl.DeviceIdType.MESH,
        )

    order = [(which, n) for which in range(3) for n in range(len(steps))]
    for which, n in order:
        pl.when(inside(*steps[n]))(lambda which=which, n=n: halo_copy(n, which).start())
    for copy in along_x:
        copy.wait_recv()
    own_copy.wait()
    along_y = [
        line_copy(
            size_x - 1 + k - 1, grid_ref.at[:, iy], grid_ref.at[:, iy],
            ix, lax.rem(iy + k, size_y),
        )
        for k in range(1, size_y)
    ]
    for copy in along_y:
        copy.start()
    for which, n in order:
        dx, dy = steps[n]
        pl.when(inside(-dx, -dy))(lambda which=which, n=n: halo_copy(n, which).wait_recv())
    for copy in along_y:
        copy.wait_recv()
    for which, n in order:
        pl.when(inside(*steps[n]))(lambda which=which, n=n: halo_copy(n, which).wait_send())
    for copy in along_x + along_y:
        copy.wait_send()


def near_kernel(
    side, count_ref, table_ref, window_ref, local_ref, out_ref, column_ref, probe_ref, result_ref
):
    wide = side + 2
    slots = window_ref.shape[3]
    quarter = slots // 4
    probes = out_ref.shape[0]
    lane = lax.broadcasted_iota(jnp.int32, (1, slots), 1)

    def prepare(cell, carry):
        x = cell // wide
        y = cell % wide
        column_ref[cell] = jnp.transpose(window_ref[x, y, probes:ROWS, :]) * UNIT
        high, low = split(window_ref[x, y, 0:probes, :] * FACTOR)
        probe_ref[cell] = jnp.concatenate([high, low], axis=0)
        return carry

    lax.fori_loop(0, wide * wide, prepare, 0)

    def one_leaf(leaf, carry):
        i = leaf // side
        j = leaf % side
        center = (i + 1) * wide + j + 1
        coords = window_ref[i + 1, j + 1, probes : probes + 2, :]
        far = jnp.dot(
            local_ref[i, j], leaf_weights(coords, table_ref), precision=HIGHEST,
            preferred_element_type=jnp.float32,
        )
        scaled_x = coords[0:1] * UNIT
        scaled_y = coords[1:2] * UNIT

        def near_part(targets):
            def one_neighbour(n, total):
                a = n // 3
                b = n % 3
                cell = (i + a) * wide + j + b
                row_x = scaled_x[:, :targets] - (a - 1).astype(jnp.float32) * UNIT
                row_y = scaled_y[:, :targets] - (b - 1).astype(jnp.float32) * UNIT

                def from_slots(size):
                    delta_x = row_x - column_ref[cell, 0:size, 0:1]
                    delta_y = row_y - column_ref[cell, 0:size, 1:2]
                    high, low = split(matern(delta_x * delta_x + delta_y * delta_y))
                    both = dot(probe_ref[cell, :, 0:size], high)
                    return (
                        total
                        + both[:probes]
                        + both[probes:]
                        + dot(probe_ref[cell, :probes, 0:size], low)
                    )

                used = (count_ref[cell] + quarter - 1) // quarter
                return lax.switch(
                    used,
                    [lambda: total]
                    + [functools.partial(from_slots, quarter * k) for k in range(1, 5)],
                )

            value = lax.fori_loop(
                0, 9, one_neighbour, jnp.zeros((probes, targets), jnp.float32)
            )
            if targets < slots:
                rest = jnp.zeros((probes, slots - targets), jnp.float32)
                value = jnp.concatenate([value, rest], axis=1)
            return value

        near = lax.cond(
            count_ref[center] > slots // 2,
            lambda: near_part(slots),
            lambda: near_part(slots // 2),
        )
        value = near + far + NUGGET * window_ref[i + 1, j + 1, 0:probes, :]
        result_ref[leaf] = jnp.where(lane < count_ref[center], value, 0.0)
        return carry

    lax.fori_loop(0, side * side, one_leaf, 0)
    for leaf in range(side * side):
        out_ref[:, leaf // side, leaf % side, :] = result_ref[leaf]


def list_tables():
    nodes = node_table() / 2.0
    node_x = np.repeat(nodes, ORDER)
    node_y = np.tile(nodes, ORDER)
    source = np.zeros((6, 6, NODES, 8))
    for x in range(6):
        for y in range(6):
            source[x, y, :, 0] = x + node_x
            source[x, y, :, 1] = y + node_y
            source[x, y, :, 2] = x
            source[x, y, :, 3] = y
    target = np.zeros((8, 2, 2, NODES))
    for x in range(2):
        for y in range(2):
            target[0, x, y] = 2 + x + node_x
            target[1, x, y] = 2 + y + node_y
            target[2, x, y] = 2 + x
            target[3, x, y] = 2 + y
    return (
        source.reshape(36 * NODES, 8).astype(np.float32),
        target.reshape(8, 4 * NODES).astype(np.float32),
    )


def matrices(target_ref, source_ref, rows, lanes, scale):
    delta_x = (target_ref[0:1, lanes] - source_ref[rows, 0:1]) * scale
    delta_y = (target_ref[1:2, lanes] - source_ref[rows, 1:2]) * scale
    apart = jnp.maximum(
        jnp.abs(target_ref[2:3, lanes] - source_ref[rows, 2:3]),
        jnp.abs(target_ref[3:4, lanes] - source_ref[rows, 3:4]),
    )
    return jnp.where(apart > 1.5, matern(delta_x * delta_x + delta_y * delta_y), 0.0)


def list_kernel(
    depth, extra, has_top, source_ref, target_ref, child_ref, maps_ref, *refs
):
    if has_top:
        top_ref, refs = refs[0], refs[1:]
    rims, grid_ref, out_ref = refs[:depth], refs[depth], refs[depth + 1]
    padded = refs[depth + 2 : depth + 2 + extra]
    locals_ref = refs[depth + 2 + extra :]
    probes = grid_ref.shape[2]
    width = target_ref.shape[1]
    groups = source_ref.shape[0] // width
    per_group = width // NODES

    for level in range(extra):
        padded[level][...] = jnp.zeros_like(padded[level])
        count_x = padded[level].shape[0] - 4
        count_y = padded[level].shape[1] - 4
        if level == 0:
            padded[0][2 : 2 + count_x, 2 : 2 + count_y] = grid_ref[...]
        else:
            for x in range(count_x):
                for y in range(count_y):
                    padded[level][2 + x, 2 + y] = merged(padded[level - 1], x, y, maps_ref, 2)

    def gathered(load, group):
        boxes = [group * per_group + n for n in range(per_group)]
        return jnp.concatenate([load(box // 6, box % 6) for box in boxes], axis=1)

    ix = lax.axis_index("gx")
    iy = lax.axis_index("gy")
    own_child = []
    for level in range(extra):
        own_child.append((ix >> level) % 2 * 2 + (iy >> level) % 2)
    lanes = slice(0, extra * NODES)
    far_target = jnp.concatenate([child_ref[child] for child in own_child], axis=1)
    lane = lax.broadcasted_iota(jnp.int32, (1, extra * NODES), 1)
    scales = jnp.zeros((1, extra * NODES), jnp.float32)
    for level in range(extra):
        scales = jnp.where(lane // NODES == level, UNIT * 2.0 ** (depth + level), scales)
    total = jnp.zeros((extra * probes, extra * NODES), jnp.float32)
    for group in range(groups):
        parts = []
        for level in range(extra):
            first_x = (ix >> (level + 1)) * 2
            first_y = (iy >> (level + 1)) * 2
            parts.append(
                gathered(lambda x, y: padded[level][first_x + x, first_y + y], group)
            )
        rows = slice(group * width, (group + 1) * width)
        matrix = matrices(far_target, source_ref, rows, lanes, scales)
        total = total + split_dot(jnp.concatenate(parts, axis=0), matrix)
    local = top_ref[...] if has_top else None
    for level in range(extra - 1, -1, -1):
        own = total[level * probes : (level + 1) * probes, level * NODES : (level + 1) * NODES]
        own = own * FACTOR
        if local is not None:
            own = own + dot_rows(local, maps_ref[own_child[level]])
        local = own
    locals_ref[depth][0, 0] = local

    for level in range(depth - 1, -1, -1):
        rim_ref = rims[level]
        half = (rim_ref.shape[0] - 4) // 2
        total = jnp.zeros((half * half * probes, width), jnp.float32)
        for group in range(groups):
            parts = [
                gathered(lambda x, y: rim_ref[2 * px + x, 2 * py + y], group)
                for px in range(half)
                for py in range(half)
            ]
            rows = slice(group * width, (group + 1) * width)
            matrix = matrices(
                target_ref, source_ref, rows, slice(0, width), UNIT * 2.0**level
            )
            total = total + split_dot(jnp.concatenate(parts, axis=0), matrix)
        target = out_ref if level == 0 else locals_ref[level]
        above = jnp.concatenate(
            [locals_ref[level + 1][px, py] for px in range(half) for py in range(half)], axis=0
        )
        for child in range(4):
            value = FACTOR * total[:, child * NODES : (child + 1) * NODES] + dot_rows(
                above, maps_ref[child]
            )
            for box in range(half * half):
                target[2 * (box // half) + child // 2, 2 * (box % half) + child % 2] = value[
                    box * probes : (box + 1) * probes
                ]


def upward(children, maps):
    half_x = children.shape[0] // 2
    half_y = children.shape[1] // 2
    grouped = children.reshape((half_x, 2, half_y, 2) + children.shape[2:])
    return jnp.einsum(
        "xyrq,ixjypr->ijpq", maps.reshape(2, 2, NODES, NODES), grouped, precision=HIGHEST
    )


def interact_top(box_grid, own_x, own_y, box_side):
    nodes = jnp.asarray(node_table() * (box_side / 2.0), jnp.float32)
    node_x = jnp.repeat(nodes, ORDER)
    node_y = jnp.tile(nodes, ORDER)
    shift_x = (jnp.arange(box_grid.shape[0], dtype=jnp.int32) - own_x).astype(jnp.float32)
    shift_y = (jnp.arange(box_grid.shape[1], dtype=jnp.int32) - own_y).astype(jnp.float32)
    delta_x = (node_x[:, None] - node_x[None, :] - shift_x[:, None, None] * box_side) * UNIT
    delta_y = (node_y[:, None] - node_y[None, :] - shift_y[:, None, None] * box_side) * UNIT
    matrices = matern((delta_x * delta_x)[:, None] + (delta_y * delta_y)[None])
    separated = jnp.maximum(jnp.abs(shift_x)[:, None], jnp.abs(shift_y)[None]) >= 2.0
    return jnp.einsum(
        "abqr,abpr->pq",
        jnp.where(separated[:, :, None, None], FACTOR * matrices, 0.0),
        box_grid,
        precision=HIGHEST,
    )


def per_device(offsets, probes, counts):
    count_p, side, _, slots = probes.shape
    depth = side.bit_length() - 1
    extra = 2
    top = depth + extra
    index_x = lax.axis_index("gx")
    index_y = lax.axis_index("gy")
    size_x = lax.axis_size("gx")
    size_y = lax.axis_size("gy")
    wide = side + 2
    table = jnp.asarray(series_at_nodes().T, jnp.float32)
    maps = jnp.asarray(child_maps())
    smem = pl.BlockSpec(memory_space=pltpu.SMEM)
    vmem = pl.BlockSpec(memory_space=pltpu.VMEM)

    def shape(*dims):
        return jax.ShapeDtypeStruct(dims, jnp.float32)

    record, *levels = pl.pallas_call(
        functools.partial(up_kernel, side),
        out_shape=[shape(side, side, ROWS, slots)]
        + [shape(side >> k, side >> k, count_p, NODES) for k in range(depth + 1)],
        in_specs=[smem, vmem, vmem, vmem, vmem],
        out_specs=[vmem] * (depth + 2),
        name="up",
    )(counts, table, maps, offsets, probes)
    window, *rims, grid = pl.pallas_call(
        functools.partial(exchange_kernel, (size_x, size_y)),
        out_shape=[shape(wide, wide, ROWS, slots)]
        + [shape((side >> k) + 4, (side >> k) + 4, count_p, NODES) for k in range(depth)]
        + [shape(size_x, size_y, count_p, NODES)],
        in_specs=[vmem] * (depth + 2),
        out_specs=[vmem] * (depth + 2),
        scratch_shapes=[
            pltpu.SemaphoreType.DMA((depth + 1, 8)),
            pltpu.SemaphoreType.DMA((depth + 1, 8)),
            pltpu.SemaphoreType.DMA((size_x + size_y - 2,)),
            pltpu.SemaphoreType.DMA((size_x + size_y - 2,)),
            pltpu.SemaphoreType.DMA,
        ],
        compiler_params=pltpu.CompilerParams(collective_id=0, has_side_effects=True),
        name="exchange",
    )(record, *levels)

    tops = []
    if max(size_x, size_y) > 2 * 2**extra:
        grids = [grid]
        for _ in range(extra):
            grids.append(upward(grids[-1], maps))
        tops = [interact_top(grids[-1], index_x // 2**extra, index_y // 2**extra, 2.0**top)]
    source_table, target_table = list_tables()
    child_table = np.ascontiguousarray(
        np.transpose(target_table.reshape(8, 4, NODES), (1, 0, 2))
    )
    local = pl.pallas_call(
        functools.partial(list_kernel, depth, extra, bool(tops)),
        out_shape=shape(side, side, count_p, NODES),
        in_specs=[vmem] * (4 + len(tops) + depth + 1),
        out_specs=vmem,
        scratch_shapes=[
            pltpu.VMEM(((size_x >> k) + 4, (size_y >> k) + 4, count_p, NODES), jnp.float32)
            for k in range(extra)
        ]
        + [
            pltpu.VMEM((side >> k, side >> k, count_p, NODES), jnp.float32)
            for k in range(depth + 1)
        ],
        name="lists",
    )(
        jnp.asarray(source_table),
        jnp.asarray(target_table),
        jnp.asarray(child_table),
        maps,
        *tops,
        *rims,
        grid,
    )
    return pl.pallas_call(
        functools.partial(near_kernel, side),
        out_shape=shape(count_p, side, side, slots),
        in_specs=[smem, vmem, vmem, vmem],
        out_specs=vmem,
        scratch_shapes=[
            pltpu.VMEM((wide * wide, slots, 8), jnp.float32),
            pltpu.VMEM((wide * wide, 2 * count_p, slots), jnp.bfloat16),
            pltpu.VMEM((side * side, count_p, slots), jnp.float32),
        ],
        name="near",
    )(
        window[:, :, count_p + 2, 0].astype(jnp.int32).reshape(wide * wide),
        table,
        window,
        local,
    )


def solution(mesh):
    placed = (P(None, "gx", "gy", None), P(None, "gx", "gy", None), P("gx", "gy"))
    return jax.shard_map(
        per_device, mesh=mesh, in_specs=placed, out_specs=P(None, "gx", "gy", None), check_vma=False
    )
```
